32 devices in a mesh: band: 8 (over y, x, core), cols: 4 (over z).
Axes of the slice: x: 2, y: 2, z: 4, core: 2. Of those that a mesh axis runs over, the one named last changes fastest.
Arguments:
- band_diagonals: float32 [256, 3072], P('cols', 'band'), may hold values from -0.4 to 0.4, as said below
- eigenvectors: float32 [3072, 512], P('band', 'cols'), may hold values from -4 to 4
Outputs:
- band_result: float32 [256, 3072], P('cols', 'band')
- transformed: float32 [3072, 512], P('band', 'cols')
The draws below stay inside these ranges and needn't reach their ends.
Inputs may be any that keep to these rules, and one draw needn't show every extreme that they name: `band_diagonals`: entry [k, r] is the matrix's entry in row r and column r - k; it is zero where k > 128 or r < k.
All inputs are finite; a program needn't handle non-finite values.
Results may differ from the reference program's by a relative error of at most 0.0003.
Values sent between devices are 32-bit elements; how exact they have to be, the bound alone decides.
A program may use at most 64 MiB of HBM per device.

```python
import jax
import jax.numpy as jnp
from jax import lax

BW = 128
SWEEPS = 4
ORDER = 3072
EIGVECS = 512


def draw_band_diagonals(key, part):
    rough = jnp.clip(jax.random.normal(key, (2 * BW, ORDER), jnp.float32), -4.0, 4.0) * 0.1
    diag_index = lax.broadcasted_iota(jnp.int32, (2 * BW, ORDER), 0)
    row_index = lax.broadcasted_iota(jnp.int32, (2 * BW, ORDER), 1)
    keep = (diag_index <= BW) & (row_index >= diag_index)
    return jnp.where(keep, rough, 0.0)


def levels(stream_key, shape, pieces, least, high):
    loudness, own = 1.0, jax.random.fold_in(stream_key, 6)
    for position, blocks in pieces:
        steps = jnp.exp(jax.random.uniform(jax.random.fold_in(own, position), (blocks,), jnp.float32, least / len(pieces), high / len(pieces)))
        loudness = loudness * jnp.repeat(steps, shape[position] // blocks).reshape([-1 if axis == position else 1 for axis in range(len(shape))])
    return loudness


def noise(stream_key, extent, spread, bound, cuts=(), kind=jnp.bfloat16):
    drawn = jax.random.normal(stream_key, extent, jnp.float32) * spread
    if len(cuts) > 0:
        drawn = levels(stream_key, extent, cuts, -0.22, 0.18) * drawn
    return jnp.clip(drawn, min=-bound, max=bound).astype(kind)


def setup_inputs(seed: int = 0) -> dict:
    key_list = jax.random.split(jax.random.key(seed), 3)
    band_diagonals = draw_band_diagonals(jax.random.fold_in(key_list[2], 71), 0)
    eigenvectors = noise(key_list[1], (ORDER, EIGVECS), 1.0, 4.0, ((0, 8), (1, 4)), jnp.float32)
    return {"band_diagonals": band_diagonals, "eigenvectors": eigenvectors}


HIGHEST = lax.Precision.HIGHEST

def skew_rows(block_rows):
    row_count, col_count = block_rows.shape
    flipped = block_rows[:, ::-1]
    padded = jnp.pad(flipped, ((0, 0), (0, row_count)))
    flat_cells = padded.reshape(-1)[:row_count * (col_count + row_count - 1)]
    return flat_cells.reshape(row_count, col_count + row_count - 1)

def unskew_rows(dense_rows, col_count):
    row_count = dense_rows.shape[0]
    flat_cells = jnp.pad(dense_rows.reshape(-1), (0, row_count))
    grid_cells = flat_cells.reshape(row_count, col_count + row_count)
    return grid_cells[:, :col_count][:, ::-1]

def chase_step(region, first_step):
    double = region.shape[0]
    half_width = double // 2
    dense_rows = skew_rows(region)
    offset = half_width - 1
    upper_rows = dense_rows[:half_width, offset:offset + double]
    lower_rows = dense_rows[half_width:, offset + half_width:offset + double]
    left_part = upper_rows[:, :half_width]
    window = upper_rows[:, half_width:]
    column = jnp.where(first_step, left_part[:, half_width - 1], left_part[:, 0])
    length = jnp.sqrt(jnp.sum(column * column))
    vector = column.at[0].add(length)
    factor = 2.0 / jnp.sum(vector * vector)
    mirror = window + window.T - jnp.diag(jnp.diag(window))
    across = factor * jnp.dot(vector, left_part, precision=HIGHEST)
    inside = factor * jnp.dot(mirror, vector, precision=HIGHEST)
    beneath = factor * jnp.dot(lower_rows, vector, precision=HIGHEST)
    inside = inside - 0.5 * factor * jnp.dot(vector, inside, precision=HIGHEST) * vector
    left_part = left_part - vector[:, None] * across[None, :]
    window = window - jnp.tril(vector[:, None] * inside[None, :] + inside[:, None] * vector[None, :])
    lower_rows = lower_rows - beneath[:, None] * vector[None, :]
    cleared = jnp.zeros_like(column).at[0].set(-length)
    left_part = jnp.where(first_step, left_part.at[:, half_width - 1].set(cleared), left_part.at[:, 0].set(cleared))
    dense_rows = dense_rows.at[:half_width, offset:offset + double].set(jnp.concatenate([left_part, window], 1))
    dense_rows = dense_rows.at[half_width:, offset + half_width:offset + double].set(lower_rows)
    return (unskew_rows(dense_rows, double), vector, factor)

def reference(band_diagonals, eigenvectors):
    band_rows = band_diagonals.T
    step_count = ORDER // BW - 2
    kept_vectors = []
    kept_factors = []
    for sweep_number in range(SWEEPS):

        def advance(carry, step_index):
            anchor = (sweep_number + 1 + step_index * BW).astype(jnp.int32)
            region = lax.dynamic_slice_in_dim(carry, anchor, 2 * BW, 0)
            region, vector, factor = chase_step(region, step_index == 0)
            carry = lax.dynamic_update_slice_in_dim(carry, region, anchor, 0)
            return (carry, (vector, factor))
        band_rows, (sweep_vectors, sweep_factors) = lax.scan(advance, band_rows, jnp.arange(step_count, dtype=jnp.int32))
        kept_vectors.append(sweep_vectors)
        kept_factors.append(sweep_factors)
    result = eigenvectors
    for sweep_number in reversed(range(SWEEPS)):
        lead_rows = sweep_number + 1
        sweep_vectors = kept_vectors[sweep_number]
        sweep_factors = kept_factors[sweep_number]
        blocks = result[lead_rows:lead_rows + step_count * BW].reshape(step_count, BW, EIGVECS)
        inner_sums = jnp.einsum('kb,kbc->kc', sweep_vectors, blocks, precision=HIGHEST)
        blocks = blocks - (sweep_factors[:, None] * sweep_vectors)[:, :, None] * inner_sums[:, None, :]
        result = result.at[lead_rows:lead_rows + step_count * BW].set(blocks.reshape(step_count * BW, EIGVECS))
    return (band_rows.T, result)
```

```python
import functools

import jax
import jax.numpy as jnp
from jax import lax
from jax.experimental import pallas as pl
from jax.experimental.pallas import tpu as pltpu
from jax.sharding import PartitionSpec as P

SWEEPS = 4
LAG = 3


def chase_kernel(blocks, half, blocks_dev, halo, piece_count, sweeps, *refs):
    band_ref, eig_ref, band_out, eig_out = refs[:4]
    d_refs = refs[4 : 5 + sweeps]
    l_refs = refs[5 + sweeps : 6 + 2 * sweeps]
    v_refs = refs[6 + 2 * sweeps : 6 + 3 * sweeps]
    tau_refs = refs[6 + 3 * sweeps : 6 + 4 * sweeps]
    x_refs = refs[6 + 4 * sweeps : 6 + 5 * sweeps]
    edge_ref, rest_ref, turn_ref = refs[6 + 5 * sweeps :]
    steps = blocks - 2
    row = lax.broadcasted_iota(jnp.int32, (half, half), 0)
    col = lax.broadcasted_iota(jnp.int32, (half, half), 1)
    lane = lax.broadcasted_iota(jnp.int32, (1, half), 1)
    eye = row == col
    row8 = lax.broadcasted_iota(jnp.int32, (8, half), 0)
    col8 = lax.broadcasted_iota(jnp.int32, (8, half), 1)
    zero = jnp.zeros((half, half), jnp.float32)

    def slot(k):
        return jnp.clip(k, -1, blocks + 1) + 1

    def unpack(block):
        dev = block // blocks_dev
        part = block % blocks_dev
        start = pl.multiple_of(part * half, half)
        piece = band_ref[dev, :half, pl.ds(start, half)]
        extra = band_ref[dev, half : half + 1, pl.ds(start, half)]
        rows = pltpu.roll(piece.T, 0, 1, stride=1, stride_axis=0)
        d_refs[0][slot(block)] = jnp.where(row >= col, rows, rows.T)
        l_refs[0][slot(block - 1)] = jnp.where(
            col > row, rows, jnp.where(eye, jnp.broadcast_to(extra, (half, half)), 0.0)
        )

    def unpack_step(block, carry):
        unpack(block)
        return carry

    lax.fori_loop(0, blocks, unpack_step, 0)
    for extra_block in (blocks, blocks + 1):
        d_refs[0][extra_block + 1] = zero
    for extra_block in (blocks - 1, blocks, blocks + 1):
        l_refs[0][extra_block + 1] = zero
    edge_ref[...] = jnp.zeros(edge_ref.shape, jnp.float32)
    rest_ref[...] = zero

    def chain(s, t):
        k = t - LAG * s
        here, after, before = slot(k), slot(k + 1), slot(k - 1)
        old, new = s, s + 1
        d_prev, l_prev, d_now, l_now = d_refs[s], l_refs[s], d_refs[s + 1], l_refs[s + 1]
        active = (k >= 0) & (k < steps)
        limit = jnp.where(active, half, 0)
        pick = jnp.where(active, new, -1)
        x = x_refs[s][...]
        d_old, l_old, d_next = d_prev[here], l_prev[here], d_prev[after]
        l_next = l_prev[after, old : old + 1, :]
        left = l_now[before]

        lead = jnp.where(lane == old, d_next[old : old + 1, :], l_old[old : old + 1, :])
        lead_col = jnp.sum(
            jnp.where(eye, jnp.broadcast_to(lead, (half, half)), 0.0), axis=1, keepdims=True
        )
        window = jnp.where(row == old, lead, jnp.where(col == old, lead_col, d_old))
        rest_row = rest_ref[old : old + 1, :]
        feed = jnp.where(k == steps - 2, half, 0)
        corner = jnp.where(lane == old, l_next, jnp.where(lane < feed, rest_row, 0.0))
        if s > 0:
            rest_ref[...] = jnp.where(
                col == jnp.where(k == steps - 1, old, -1), l_old, rest_ref[...]
            )
        below = jnp.where(row == old, corner, jnp.where(col == old, d_next, l_old))

        rest = jnp.sum(jnp.where(row == new, 0.0, x * x), axis=0, keepdims=True)
        top = x[new : new + 1, :]
        length = jnp.sqrt(rest + top * top)
        v_top = top + length
        tau = 2.0 / (rest + v_top * v_top)
        tau = jnp.where(lane < limit, tau, 0.0)
        v_col = jnp.where(row < limit, jnp.where(row == new, v_top, x), 0.0)
        v_row = jnp.sum(jnp.where(eye, v_col, 0.0), axis=0, keepdims=True)

        beneath = jnp.sum(below * v_row, axis=1, keepdims=True)
        beneath = jnp.where(row < limit, beneath * tau, 0.0)
        first = k < 0
        source = jnp.where(first, old, new)
        head = jnp.where(row == old, l_next, d_next)
        early = jnp.where(first, half, 0)
        column = jnp.where(row < early, head, below)
        column = jnp.sum(jnp.where(col == source, column, 0.0), axis=1, keepdims=True)
        x_refs[s][...] = column - jnp.where(row < limit, beneath * v_top, 0.0)
        below = below - beneath * v_row

        inside = tau * jnp.sum(v_col * window, axis=0, keepdims=True)
        scale = 0.5 * tau * jnp.sum(v_row * inside, axis=1, keepdims=True)
        z_row = inside - scale * v_row
        z_col = jnp.sum(
            jnp.where(eye, jnp.broadcast_to(z_row, (half, half)), 0.0), axis=1, keepdims=True
        )
        window = window - v_col * z_row - z_col * v_row

        across = tau * jnp.sum(v_col * left, axis=0, keepdims=True)
        left = left - v_col * across
        left = jnp.where(col == pick, jnp.where(row == new, -length, 0.0), left)

        l_now[before] = left
        d_now[here] = window
        l_now[here] = below
        v_refs[s][here] = v_col
        tau_refs[s][here] = jnp.broadcast_to(tau, (8, half))

        start = jnp.where(k == 0, s, -1)
        edge = edge_ref[...]
        edge = jnp.where((row8 == start) & (col8 == s), d_old[:8], edge)
        below_start = jnp.where(k == 0, s + 1, -1)
        edge = jnp.where((row8 == below_start) & (col8 == s), -length, edge)
        edge_ref[...] = edge

    def wave(t, carry):
        for s in reversed(range(sweeps)):
            chain(s, t)
        return carry

    lax.fori_loop(-1, blocks + LAG * (sweeps - 1), wave, 0)

    device = lax.axis_index("band")
    base = device * blocks_dev - halo
    eig = [eig_ref[e * half : (e + 1) * half, :] for e in range(halo + blocks_dev)]
    eig.append(eig_ref[(halo + blocks_dev) * half : (halo + blocks_dev) * half + 8, :])
    for s in reversed(range(sweeps)):
        lead_rows = s + 1
        for e in range(sweeps - 1 - s + halo - sweeps, halo + blocks_dev):
            k = base + e
            v = v_refs[s][slot(k)]
            tau = tau_refs[s][slot(k), 0:1, :]
            low, high = eig[e], eig[e + 1]
            mixed = jnp.concatenate([jnp.where(row8 < lead_rows, high[:8], low[:8]), low[8:]], 0)
            inner = tau * jnp.sum(v * mixed, axis=0, keepdims=True)
            mixed = mixed - v * inner
            eig[e] = jnp.concatenate([jnp.where(row8 < lead_rows, low[:8], mixed[:8]), mixed[8:]], 0)
            top = jnp.where(row8 < lead_rows, mixed[:8], high[:8])
            eig[e + 1] = jnp.concatenate([top, high[8:]], 0) if high.shape[0] > 8 else top
    for m in range(blocks_dev):
        eig_out[m * half : (m + 1) * half, :] = eig[halo + m]

    d_last, l_last = d_refs[sweeps], l_refs[sweeps]
    edge = jnp.concatenate([edge_ref[...], zero[8:]], axis=0)
    rest = rest_ref[...]
    d_last[0] = jnp.where(row < sweeps, edge, 0.0)
    l_last[0] = jnp.where(row >= sweeps, edge, 0.0)
    flip = jnp.where((row + col == half) | ((row == 0) & (col == 0)), 1.0, 0.0)
    position = lax.axis_index("cols") * piece_count
    for m in range(blocks_dev):
        b = device * blocks_dev + m
        lim = jnp.where(b > 0, half, 0)
        rest_below = jnp.where(b == steps, half, 0)
        rest_last = jnp.where(b == steps + 1, half, 0)
        d_here, d_before = d_last[slot(b)], d_last[slot(b - 1)]
        l_here, l_before = l_last[slot(b - 1)], l_last[slot(b - 2)]
        c0 = jnp.where(
            row >= sweeps, jnp.where(col >= sweeps, d_here, l_here), jnp.where(col < sweeps, d_before, 0.0)
        )
        c1 = jnp.where(
            row >= sweeps,
            jnp.where(col >= sweeps, l_here, jnp.where(row < rest_below, rest, 0.0)),
            jnp.where(col >= sweeps, d_before, l_before),
        )
        c1 = jnp.where(row < lim, c1, 0.0)
        c2 = jnp.where(col >= sweeps, l_before, jnp.where(row < rest_last, rest, 0.0))
        c2 = jnp.where(row < sweeps, c2, 0.0)
        c2 = jnp.where(row < lim, c2, 0.0)
        lower = jnp.where(col <= row, c0, c1)
        upper = jnp.where(col <= row, c1, c2)
        for n, part in enumerate((lower, upper)):
            turned = jnp.dot(part, flip, precision=lax.Precision.HIGHEST)
            turned = pltpu.roll(turned, 0, 1, stride=1, stride_axis=0)
            turn_ref[n * half : (n + 1) * half, :] = turned.T
        band_out[:, m * half : (m + 1) * half] = turn_ref[pl.ds(pl.multiple_of(position, 8), piece_count), :]


def shifted(x, axis, by):
    peers = lax.axis_size(axis)
    pairs = [(i, i + by) for i in range(peers) if 0 <= i + by < peers]
    return lax.ppermute(x, axis, pairs)


def body(band_diagonals, eigenvectors):
    piece_count, rows_dev = band_diagonals.shape
    double = piece_count * lax.axis_size("cols")
    half = double // 2
    blocks_dev = rows_dev // half
    devices = lax.axis_size("band")
    blocks = blocks_dev * devices
    sweeps = SWEEPS
    pieces = lax.all_gather(band_diagonals, "cols", axis=0, tiled=True)
    turned = jnp.concatenate(
        [pieces[:1], pieces[half - 1 : 0 : -1], pieces[half : half + 8]], axis=0
    )
    band = lax.all_gather(turned, "band", axis=0, tiled=False)

    halo = sweeps
    parts = []
    need = halo * half
    hop = 1
    while need > 0:
        take = min(need, rows_dev)
        parts.insert(0, shifted(eigenvectors[rows_dev - take :], "band", hop))
        need -= take
        hop += 1
    parts.append(eigenvectors)
    parts.append(shifted(eigenvectors[:8], "band", -1))
    eig = jnp.concatenate(parts, axis=0)
    columns = eigenvectors.shape[1]

    slots = blocks + 3
    f32 = jnp.float32
    scratch = (
        [pltpu.VMEM((slots, half, half), f32)] * (2 * (sweeps + 1))
        + [pltpu.VMEM((slots, half, half), f32)] * sweeps
        + [pltpu.VMEM((slots, 8, half), f32)] * sweeps
        + [pltpu.VMEM((half, half), f32)] * sweeps
        + [
            pltpu.VMEM((8, half), f32),
            pltpu.VMEM((half, half), f32),
            pltpu.VMEM((double, half), f32),
        ]
    )
    vmem = pl.BlockSpec(memory_space=pltpu.VMEM)
    return pl.pallas_call(
        functools.partial(chase_kernel, blocks, half, blocks_dev, halo, piece_count, sweeps),
        out_shape=(
            jax.ShapeDtypeStruct((piece_count, rows_dev), f32),
            jax.ShapeDtypeStruct((rows_dev, columns), f32),
        ),
        in_specs=[vmem, vmem],
        out_specs=(vmem, vmem),
        scratch_shapes=scratch,
        compiler_params=pltpu.CompilerParams(vmem_limit_bytes=62 * 1024 * 1024),
    )(band, eig)


def solution(mesh):
    return jax.shard_map(
        body,
        mesh=mesh,
        in_specs=(P("cols", "band"), P("band", "cols")),
        out_specs=(P("cols", "band"), P("band", "cols")),
        check_vma=False,
    )
```

```python
import functools

import jax
import jax.numpy as jnp
from jax import lax
from jax.experimental import pallas as pl
from jax.experimental.pallas import tpu as pltpu
from jax.sharding import PartitionSpec as P

SWEEPS = 4
LAG = 3


def chase_kernel(blocks, half, blocks_dev, halo, piece_count, sweeps, *refs):
    band_ref, above_ref, eig_ref, under_ref, band_out, eig_out = refs[:6]
    refs = refs[2:]
    d_refs = refs[4 : 5 + sweeps]
    l_refs = refs[5 + sweeps : 6 + 2 * sweeps]
    v_refs = refs[6 + 2 * sweeps : 6 + 3 * sweeps]
    tau_refs = refs[6 + 3 * sweeps : 6 + 4 * sweeps]
    x_refs = refs[6 + 4 * sweeps : 6 + 5 * sweeps]
    edge_ref, rest_ref, turn_ref = refs[6 + 5 * sweeps :]
    steps = blocks - 2
    row = lax.broadcasted_iota(jnp.int32, (half, half), 0)
    col = lax.broadcasted_iota(jnp.int32, (half, half), 1)
    lane = lax.broadcasted_iota(jnp.int32, (1, half), 1)
    eye = row == col
    row8 = lax.broadcasted_iota(jnp.int32, (8, half), 0)
    col8 = lax.broadcasted_iota(jnp.int32, (8, half), 1)
    zero = jnp.zeros((half, half), jnp.float32)

    def slot(k):
        return jnp.clip(k, -1, blocks + 1) + 1

    def unpack(block):
        dev = block // blocks_dev
        part = block % blocks_dev
        start = pl.multiple_of(part * half, half)
        piece = band_ref[dev, :half, pl.ds(start, half)]
        extra = band_ref[dev, half : half + 1, pl.ds(start, half)]
        rows = pltpu.roll(piece.T, 1, 1, stride=1, stride_axis=0)
        d_refs[0][slot(block)] = jnp.where(row >= col, rows, rows.T)
        l_refs[0][slot(block - 1)] = jnp.where(
            col > row, rows, jnp.where(eye, jnp.broadcast_to(extra, (half, half)), 0.0)
        )

    def unpack_step(block, carry):
        unpack(block)
        return carry

    lax.fori_loop(0, blocks, unpack_step, 0)
    for extra_block in (blocks, blocks + 1):
        d_refs[0][extra_block + 1] = zero
    for extra_block in (blocks - 1, blocks, blocks + 1):
        l_refs[0][extra_block + 1] = zero
    edge_ref[...] = jnp.zeros(edge_ref.shape, jnp.float32)
    rest_ref[...] = zero

    def chain(s, t):
        k = t - LAG * s
        here, after, before = slot(k), slot(k + 1), slot(k - 1)
        old, new = s, s + 1
        d_prev, l_prev, d_now, l_now = d_refs[s], l_refs[s], d_refs[s + 1], l_refs[s + 1]
        active = (k >= 0) & (k < steps)
        limit = jnp.where(active, half, 0)
        pick = jnp.where(active, new, -1)
        x = x_refs[s][...]
        d_old, l_old, d_next = d_prev[here], l_prev[here], d_prev[after]
        l_next = l_prev[after, old : old + 1, :]
        left = l_now[before]

        lead = jnp.where(lane == old, d_next[old : old + 1, :], l_old[old : old + 1, :])
        lead_col = jnp.sum(
            jnp.where(eye, jnp.broadcast_to(lead, (half, half)), 0.0), axis=1, keepdims=True
        )
        window = jnp.where(row == old, lead, jnp.where(col == old, lead_col, d_old))
        rest_row = rest_ref[old : old + 1, :]
        feed = jnp.where(k == steps - 2, half, 0)
        corner = jnp.where(lane == old, l_next, jnp.where(lane < feed, rest_row, 0.0))
        if s > 0:
            rest_ref[...] = jnp.where(
                col == jnp.where(k == steps - 1, old, -1), l_old, rest_ref[...]
            )
        below = jnp.where(row == old, corner, jnp.where(col == old, d_next, l_old))

        rest = jnp.sum(jnp.where(row == new, 0.0, x * x), axis=0, keepdims=True)
        top = x[new : new + 1, :]
        length = jnp.sqrt(rest + top * top)
        v_top = top + length
        tau = 2.0 / (rest + v_top * v_top)
        tau = jnp.where(lane < limit, tau, 0.0)
        v_col = jnp.where(row < limit, jnp.where(row == new, v_top, x), 0.0)
        v_row = jnp.sum(jnp.where(eye, v_col, 0.0), axis=0, keepdims=True)

        beneath = jnp.sum(below * v_row, axis=1, keepdims=True)
        beneath = jnp.where(row < limit, beneath * tau, 0.0)
        first = k < 0
        source = jnp.where(first, old, new)
        head = jnp.where(row == old, l_next, d_next)
        early = jnp.where(first, half, 0)
        column = jnp.where(row < early, head, below)
        column = jnp.sum(jnp.where(col == source, column, 0.0), axis=1, keepdims=True)
        x_refs[s][...] = column - jnp.where(row < limit, beneath * v_top, 0.0)
        below = below - beneath * v_row

        inside = tau * jnp.sum(v_col * window, axis=0, keepdims=True)
        scale = 0.5 * tau * jnp.sum(v_row * inside, axis=1, keepdims=True)
        z_row = inside - scale * v_row
        z_col = jnp.sum(
            jnp.where(eye, jnp.broadcast_to(z_row, (half, half)), 0.0), axis=1, keepdims=True
        )
        window = window - v_col * z_row - z_col * v_row

        across = tau * jnp.sum(v_col * left, axis=0, keepdims=True)
        left = left - v_col * across
        left = jnp.where(col == pick, jnp.where(row == new, -length, 0.0), left)

        l_now[before] = left
        d_now[here] = window
        l_now[here] = below
        v_refs[s][here] = v_col
        tau_refs[s][here] = jnp.broadcast_to(tau, (8, half))

        start = jnp.where(k == 0, s, -1)
        edge = edge_ref[...]
        edge = jnp.where((row8 == start) & (col8 == s), d_old[:8], edge)
        below_start = jnp.where(k == 0, s + 1, -1)
        edge = jnp.where((row8 == below_start) & (col8 == s), -length, edge)
        edge_ref[...] = edge

    def wave(t, carry):
        for s in reversed(range(sweeps)):
            chain(s, t)
        return carry

    lax.fori_loop(-1, blocks + LAG * (sweeps - 1), wave, 0)

    device = lax.axis_index("band")
    base = device * blocks_dev - halo
    eig = [above_ref[e * half : (e + 1) * half, :] for e in range(halo)]
    eig += [eig_ref[e * half : (e + 1) * half, :] for e in range(blocks_dev)]
    eig.append(under_ref[...])
    for s in reversed(range(sweeps)):
        lead_rows = s + 1
        for e in range(sweeps - 1 - s + halo - sweeps, halo + blocks_dev):
            k = base + e
            v = v_refs[s][slot(k)]
            tau = tau_refs[s][slot(k), 0:1, :]
            low, high = eig[e], eig[e + 1]
            mixed = jnp.concatenate([jnp.where(row8 < lead_rows, high[:8], low[:8]), low[8:]], 0)
            inner = tau * jnp.sum(v * mixed, axis=0, keepdims=True)
            mixed = mixed - v * inner
            eig[e] = jnp.concatenate([jnp.where(row8 < lead_rows, low[:8], mixed[:8]), mixed[8:]], 0)
            top = jnp.where(row8 < lead_rows, mixed[:8], high[:8])
            eig[e + 1] = jnp.concatenate([top, high[8:]], 0) if high.shape[0] > 8 else top
    for m in range(blocks_dev):
        eig_out[m * half : (m + 1) * half, :] = eig[halo + m]

    d_last, l_last = d_refs[sweeps], l_refs[sweeps]
    edge = jnp.concatenate([edge_ref[...], zero[8:]], axis=0)
    rest = rest_ref[...]
    d_last[0] = jnp.where(row < sweeps, edge, 0.0)
    l_last[0] = jnp.where(row >= sweeps, edge, 0.0)
    flip = jnp.where((row + col == half) | ((row == 0) & (col == 0)), 1.0, 0.0)
    position = lax.axis_index("cols") * piece_count
    for m in range(blocks_dev):
        b = device * blocks_dev + m
        lim = jnp.where(b > 0, half, 0)
        rest_below = jnp.where(b == steps, half, 0)
        rest_last = jnp.where(b == steps + 1, half, 0)
        d_here, d_before = d_last[slot(b)], d_last[slot(b - 1)]
        l_here, l_before = l_last[slot(b - 1)], l_last[slot(b - 2)]
        c0 = jnp.where(
            row >= sweeps, jnp.where(col >= sweeps, d_here, l_here), jnp.where(col < sweeps, d_before, 0.0)
        )
        c1 = jnp.where(
            row >= sweeps,
            jnp.where(col >= sweeps, l_here, jnp.where(row < rest_below, rest, 0.0)),
            jnp.where(col >= sweeps, d_before, l_before),
        )
        c1 = jnp.where(row < lim, c1, 0.0)
        c2 = jnp.where(col >= sweeps, l_before, jnp.where(row < rest_last, rest, 0.0))
        c2 = jnp.where(row < sweeps, c2, 0.0)
        c2 = jnp.where(row < lim, c2, 0.0)
        lower = jnp.where(col <= row, c0, c1)
        upper = jnp.where(col <= row, c1, c2)
        for n, part in enumerate((lower, upper)):
            turned = jnp.dot(part, flip, precision=lax.Precision.HIGHEST)
            turned = pltpu.roll(turned, 0, 1, stride=1, stride_axis=0)
            turn_ref[n * half : (n + 1) * half, :] = turned.T
        band_out[:, m * half : (m + 1) * half] = turn_ref[pl.ds(pl.multiple_of(position, 8), piece_count), :]


def gather_kernel(half, devices, cols, takes, rev_ref, band_ref, eig_ref, all_ref, above_ref, under_ref, sems):
    z_send, z_recv, p_send, p_recv, c_send, c_recv, e_send, e_recv, own_sem = sems
    d, c = lax.axis_index("band"), lax.axis_index("cols")
    count = rev_ref.shape[0]
    full = half // count
    pieces = full + 1
    chips = devices // 2
    chip, core = d // 2, d % 2
    partner = chip * 2 + 1 - core

    def at(rel):
        return (chip + rel + chips) % chips * 2 + core

    barrier = pltpu.get_barrier_semaphore()
    peers = [(d, (c + i) % cols) for i in range(1, cols)]
    peers += [(at(i), c) for i in range(1, chips)]
    peers.append((partner, c))
    for hop in range(1, len(takes) + 1):
        peers += [((d + hop) % devices, c), ((d - hop + devices) % devices, c)]
    for peer in peers:
        pl.semaphore_signal(barrier, inc=1, device_id=peer, device_id_type=pl.DeviceIdType.MESH)
    pl.semaphore_wait(barrier, len(peers))

    def send(src, dst, send_sem, recv_sem, device):
        return pltpu.make_async_remote_copy(
            src_ref=src,
            dst_ref=dst,
            send_sem=send_sem,
            recv_sem=recv_sem,
            device_id=device,
            device_id_type=pl.DeviceIdType.MESH,
        )

    def place(dev, p):
        if p < full:
            return all_ref.at[dev, pl.ds(half - (p + 1) * count, count)]
        return all_ref.at[dev, pl.ds(half, 8)]

    def source(p):
        return rev_ref if p < full else band_ref.at[pl.ds(0, 8)]

    def along(p, i):
        return send(source(p), place(d, p), z_send.at[p, i], z_recv.at[p], (d, (c + i) % cols))

    def across(p, i, src):
        return send(src, place(d, p), p_send.at[p, i], p_recv.at[p, i], (at(i), c))

    def pair(p, i, src, dev):
        return send(src, place(dev, p), c_send.at[p, i], c_recv.at[p, i], (partner, c))

    def own(p):
        return pltpu.make_async_copy(source(p), place(d, p), own_sem)

    rows_dev = eig_ref.shape[0]
    total = sum(takes)
    halos = []
    end = total
    for hop, take in enumerate(takes, 1):
        halos.append(
            send(
                eig_ref.at[pl.ds(rows_dev - take, take)],
                above_ref.at[pl.ds(end - take, take)],
                e_send.at[hop],
                e_recv.at[hop],
                ((d + hop) % devices, c),
            )
        )
        end -= take
    halos.append(
        send(eig_ref.at[pl.ds(0, 8)], under_ref, e_send.at[0], e_recv.at[0], ((d - 1 + devices) % devices, c))
    )

    for p in range(pieces):

        @pl.when(c == p)
        def _():
            for i in range(1, cols):
                along(p, i).start()
            for i in range(1, chips):
                across(p, i, source(p)).start()
            pair(p, 0, source(p), d).start()
            own(p).start()

    for p in range(pieces):

        @pl.when(c != p)
        def _():
            along(p, 1).wait_recv()
            for i in range(1, chips):
                across(p, i, place(d, p)).start()
            pair(p, 0, place(d, p), d).start()

    for halo in halos:
        halo.start()
    for i in range(1, chips):
        for p in range(pieces):
            across(p, i, place(d, p)).wait_recv()
            pair(p, i, place(at(-i), p), at(-i)).start()
    for p in range(pieces):

        @pl.when(c == p)
        def _():
            own(p).wait()
            for i in range(1, cols):
                along(p, i).wait_send()

    for p in range(pieces):
        for i in range(1, chips):
            across(p, i, place(d, p)).wait_send()
        for i in range(chips):
            pair(p, i, place(at(-i), p), at(-i)).wait()
    for halo in halos:
        halo.wait()


def body(band_diagonals, eigenvectors):
    piece_count, rows_dev = band_diagonals.shape
    cols = lax.axis_size("cols")
    double = piece_count * cols
    half = double // 2
    blocks_dev = rows_dev // half
    devices = lax.axis_size("band")
    blocks = blocks_dev * devices
    sweeps = SWEEPS
    halo = sweeps
    columns = eigenvectors.shape[1]
    f32 = jnp.float32
    vmem = pl.BlockSpec(memory_space=pltpu.VMEM)

    takes = []
    while sum(takes) < halo * half:
        takes.append(min(halo * half - sum(takes), rows_dev))
    pieces = half // piece_count + 1
    dma = pltpu.SemaphoreType.DMA
    band, above, under = pl.pallas_call(
        functools.partial(gather_kernel, half, devices, cols, takes),
        out_shape=(
            jax.ShapeDtypeStruct((devices, half + 8, rows_dev), f32),
            jax.ShapeDtypeStruct((halo * half, columns), f32),
            jax.ShapeDtypeStruct((8, columns), f32),
        ),
        in_specs=[vmem] * 3,
        out_specs=(vmem,) * 3,
        scratch_shapes=[
            [
                dma((pieces, cols)),
                dma((pieces,)),
                dma((pieces, devices)),
                dma((pieces, devices)),
                dma((pieces, devices)),
                dma((pieces, devices)),
                dma((len(takes) + 1,)),
                dma((len(takes) + 1,)),
                dma,
            ]
        ],
        compiler_params=pltpu.CompilerParams(collective_id=0, has_side_effects=True),
    )(band_diagonals[::-1], band_diagonals, eigenvectors)

    slots = blocks + 3
    scratch = (
        [pltpu.VMEM((slots, half, half), f32)] * (2 * (sweeps + 1))
        + [pltpu.VMEM((slots, half, half), f32)] * sweeps
        + [pltpu.VMEM((slots, 8, half), f32)] * sweeps
        + [pltpu.VMEM((half, half), f32)] * sweeps
        + [
            pltpu.VMEM((8, half), f32),
            pltpu.VMEM((half, half), f32),
            pltpu.VMEM((double, half), f32),
        ]
    )
    return pl.pallas_call(
        functools.partial(chase_kernel, blocks, half, blocks_dev, halo, piece_count, sweeps),
        out_shape=(
            jax.ShapeDtypeStruct((piece_count, rows_dev), f32),
            jax.ShapeDtypeStruct((rows_dev, columns), f32),
        ),
        in_specs=[vmem] * 4,
        out_specs=(vmem, vmem),
        scratch_shapes=scratch,
        compiler_params=pltpu.CompilerParams(vmem_limit_bytes=62 * 1024 * 1024),
    )(band, above, eigenvectors, under)


def solution(mesh):
    return jax.shard_map(
        body,
        mesh=mesh,
        in_specs=(P("cols", "band"), P("band", "cols")),
        out_specs=(P("cols", "band"), P("band", "cols")),
        check_vma=False,
    )
```

```python
import functools

import jax
import jax.numpy as jnp
from jax import lax
from jax.experimental import pallas as pl
from jax.experimental.pallas import tpu as pltpu
from jax.sharding import PartitionSpec as P

SWEEPS = 4
LAG = 3


def chase_kernel(blocks, half, blocks_dev, halo, piece_count, sweeps, *refs):
    band_ref, above_ref, eig_ref, under_ref, band_out, eig_out = refs[:6]
    refs = refs[2:]
    d_refs = refs[4 : 5 + sweeps]
    l_refs = refs[5 + sweeps : 6 + 2 * sweeps]
    v_refs = refs[6 + 2 * sweeps : 6 + 3 * sweeps]
    tau_refs = refs[6 + 3 * sweeps : 6 + 4 * sweeps]
    x_refs = refs[6 + 4 * sweeps : 6 + 5 * sweeps]
    edge_ref, rest_ref, turn_ref = refs[6 + 5 * sweeps :]
    steps = blocks - 2
    row = lax.broadcasted_iota(jnp.int32, (half, half), 0)
    col = lax.broadcasted_iota(jnp.int32, (half, half), 1)
    lane = lax.broadcasted_iota(jnp.int32, (1, half), 1)
    eye = row == col
    row8 = lax.broadcasted_iota(jnp.int32, (8, half), 0)
    col8 = lax.broadcasted_iota(jnp.int32, (8, half), 1)
    zero = jnp.zeros((half, half), jnp.float32)

    def slot(k):
        return jnp.clip(k, -1, blocks + 1) + 1

    def unpack(block):
        dev = block // blocks_dev
        part = block % blocks_dev
        start = pl.multiple_of(part * half, half)
        piece = band_ref[dev, :half, pl.ds(start, half)]
        extra = band_ref[dev, half : half + 1, pl.ds(start, half)]
        rows = pltpu.roll(piece.T, 1, 1, stride=1, stride_axis=0)
        d_refs[0][slot(block)] = jnp.where(row >= col, rows, rows.T)
        l_refs[0][slot(block - 1)] = jnp.where(
            col > row, rows, jnp.where(eye, jnp.broadcast_to(extra, (half, half)), 0.0)
        )

    def unpack_step(block, carry):
        unpack(block)
        return carry

    lax.fori_loop(0, blocks, unpack_step, 0)
    for extra_block in (blocks, blocks + 1):
        d_refs[0][extra_block + 1] = zero
    for extra_block in (blocks - 1, blocks, blocks + 1):
        l_refs[0][extra_block + 1] = zero
    edge_ref[...] = jnp.zeros(edge_ref.shape, jnp.float32)
    rest_ref[...] = zero

    def chain(s, t):
        k = t - LAG * s
        here, after, before = slot(k), slot(k + 1), slot(k - 1)
        old, new = s, s + 1
        d_prev, l_prev, d_now, l_now = d_refs[s], l_refs[s], d_refs[s + 1], l_refs[s + 1]
        active = (k >= 0) & (k < steps)
        limit = jnp.where(active, half, 0)
        pick = jnp.where(active, new, -1)
        x = x_refs[s][...]
        d_old, l_old, d_next = d_prev[here], l_prev[here], d_prev[after]
        l_next = l_prev[after, old : old + 1, :]
        left = l_now[before]

        lead = jnp.where(lane == old, d_next[old : old + 1, :], l_old[old : old + 1, :])
        lead_col = jnp.sum(
            jnp.where(eye, jnp.broadcast_to(lead, (half, half)), 0.0), axis=1, keepdims=True
        )
        window = jnp.where(row == old, lead, jnp.where(col == old, lead_col, d_old))
        rest_row = rest_ref[old : old + 1, :]
        feed = jnp.where(k == steps - 2, half, 0)
        corner = jnp.where(lane == old, l_next, jnp.where(lane < feed, rest_row, 0.0))
        if s > 0:
            rest_ref[...] = jnp.where(
                col == jnp.where(k == steps - 1, old, -1), l_old, rest_ref[...]
            )
        below = jnp.where(row == old, corner, jnp.where(col == old, d_next, l_old))

        rest = jnp.sum(jnp.where(row == new, 0.0, x * x), axis=0, keepdims=True)
        top = x[new : new + 1, :]
        length = jnp.sqrt(rest + top * top)
        v_top = top + length
        tau = 2.0 / (rest + v_top * v_top)
        tau = jnp.where(lane < limit, tau, 0.0)
        v_col = jnp.where(row < limit, jnp.where(row == new, v_top, x), 0.0)
        v_row = jnp.sum(jnp.where(eye, v_col, 0.0), axis=0, keepdims=True)

        beneath = jnp.sum(below * v_row, axis=1, keepdims=True)
        beneath = jnp.where(row < limit, beneath * tau, 0.0)
        first = k < 0
        source = jnp.where(first, old, new)
        head = jnp.where(row == old, l_next, d_next)
        early = jnp.where(first, half, 0)
        column = jnp.where(row < early, head, below)
        column = jnp.sum(jnp.where(col == source, column, 0.0), axis=1, keepdims=True)
        x_refs[s][...] = column - jnp.where(row < limit, beneath * v_top, 0.0)
        below = below - beneath * v_row

        inside = tau * jnp.sum(v_col * window, axis=0, keepdims=True)
        scale = 0.5 * tau * jnp.sum(v_row * inside, axis=1, keepdims=True)
        z_row = inside - scale * v_row
        z_col = jnp.sum(
            jnp.where(eye, jnp.broadcast_to(z_row, (half, half)), 0.0), axis=1, keepdims=True
        )
        window = window - v_col * z_row - z_col * v_row

        across = tau * jnp.sum(v_col * left, axis=0, keepdims=True)
        left = left - v_col * across
        left = jnp.where(col == pick, jnp.where(row == new, -length, 0.0), left)

        l_now[before] = left
        d_now[here] = window
        l_now[here] = below
        v_refs[s][here] = v_col
        tau_refs[s][here] = jnp.broadcast_to(tau, (8, half))

        start = jnp.where(k == 0, s, -1)
        edge = edge_ref[...]
        edge = jnp.where((row8 == start) & (col8 == s), d_old[:8], edge)
        below_start = jnp.where(k == 0, s + 1, -1)
        edge = jnp.where((row8 == below_start) & (col8 == s), -length, edge)
        edge_ref[...] = edge

    def wave(t, carry):
        for s in reversed(range(sweeps)):
            chain(s, t)
        return carry

    lax.fori_loop(-1, blocks + LAG * (sweeps - 1), wave, 0)

    device = lax.axis_index("band")
    base = device * blocks_dev - halo
    eig = [above_ref[e * half : (e + 1) * half, :] for e in range(halo)]
    eig += [eig_ref[e * half : (e + 1) * half, :] for e in range(blocks_dev)]
    eig.append(under_ref[...])
    for s in reversed(range(sweeps)):
        lead_rows = s + 1
        for e in range(sweeps - 1 - s + halo - sweeps, halo + blocks_dev):
            k = base + e
            v = v_refs[s][slot(k)]
            tau = tau_refs[s][slot(k), 0:1, :]
            low, high = eig[e], eig[e + 1]
            mixed = jnp.concatenate([jnp.where(row8 < lead_rows, high[:8], low[:8]), low[8:]], 0)
            inner = tau * jnp.sum(v * mixed, axis=0, keepdims=True)
            mixed = mixed - v * inner
            eig[e] = jnp.concatenate([jnp.where(row8 < lead_rows, low[:8], mixed[:8]), mixed[8:]], 0)
            top = jnp.where(row8 < lead_rows, mixed[:8], high[:8])
            eig[e + 1] = jnp.concatenate([top, high[8:]], 0) if high.shape[0] > 8 else top
    for m in range(blocks_dev):
        eig_out[m * half : (m + 1) * half, :] = eig[halo + m]

    d_last, l_last = d_refs[sweeps], l_refs[sweeps]
    edge = jnp.concatenate([edge_ref[...], zero[8:]], axis=0)
    rest = rest_ref[...]
    d_last[0] = jnp.where(row < sweeps, edge, 0.0)
    l_last[0] = jnp.where(row >= sweeps, edge, 0.0)
    flip = jnp.where((row + col == half) | ((row == 0) & (col == 0)), 1.0, 0.0)
    position = lax.axis_index("cols") * piece_count
    for m in range(blocks_dev):
        b = device * blocks_dev + m
        lim = jnp.where(b > 0, half, 0)
        rest_below = jnp.where(b == steps, half, 0)
        rest_last = jnp.where(b == steps + 1, half, 0)
        d_here, d_before = d_last[slot(b)], d_last[slot(b - 1)]
        l_here, l_before = l_last[slot(b - 1)], l_last[slot(b - 2)]
        c0 = jnp.where(
            row >= sweeps, jnp.where(col >= sweeps, d_here, l_here), jnp.where(col < sweeps, d_before, 0.0)
        )
        c1 = jnp.where(
            row >= sweeps,
            jnp.where(col >= sweeps, l_here, jnp.where(row < rest_below, rest, 0.0)),
            jnp.where(col >= sweeps, d_before, l_before),
        )
        c1 = jnp.where(row < lim, c1, 0.0)
        c2 = jnp.where(col >= sweeps, l_before, jnp.where(row < rest_last, rest, 0.0))
        c2 = jnp.where(row < sweeps, c2, 0.0)
        c2 = jnp.where(row < lim, c2, 0.0)
        lower = jnp.where(col <= row, c0, c1)
        upper = jnp.where(col <= row, c1, c2)
        for n, part in enumerate((lower, upper)):
            turned = jnp.dot(part, flip, precision=lax.Precision.HIGHEST)
            turned = pltpu.roll(turned, 0, 1, stride=1, stride_axis=0)
            turn_ref[n * half : (n + 1) * half, :] = turned.T
        band_out[:, m * half : (m + 1) * half] = turn_ref[pl.ds(pl.multiple_of(position, 8), piece_count), :]


def gather_kernel(half, devices, cols, takes, band_ref, eig_ref, all_ref, above_ref, under_ref, rev_ref, sems):
    z_send, z_recv, p_send, p_recv, c_send, c_recv, e_send, e_recv, own_sem = sems
    d, c = lax.axis_index("band"), lax.axis_index("cols")
    count = band_ref.shape[0]
    full = half // count
    pieces = full + 1
    chips = devices // 2
    tall = chips // 2
    chip, core = d // 2, d % 2
    partner = chip * 2 + 1 - core
    spot = (1 - chip % 2) * (chip // 2) + (chip % 2) * (chips - 1 - chip // 2)

    def at(rel):
        ring = (spot + rel + chips) % chips
        turn = ring // tall
        return ((1 - turn) * 2 * ring + turn * (2 * (chips - 1 - ring) + 1)) * 2 + core

    for r in range(count):
        rev_ref[r : r + 1, :] = band_ref[count - 1 - r : count - r, :]

    barrier = pltpu.get_barrier_semaphore()
    peers = [(at(1), c), (at(-1), c), (partner, c)]
    for hop in range(1, len(takes) + 1):
        peers += [((d + hop) % devices, c), ((d - hop + devices) % devices, c)]
    for peer in peers:
        pl.semaphore_signal(barrier, inc=1, device_id=peer, device_id_type=pl.DeviceIdType.MESH)

    @pl.when(c > 0)
    def _():
        pl.semaphore_signal(barrier, inc=1, device_id=(d, c - 1), device_id_type=pl.DeviceIdType.MESH)

    @pl.when(c < cols - 1)
    def _():
        pl.semaphore_signal(barrier, inc=1, device_id=(d, c + 1), device_id_type=pl.DeviceIdType.MESH)

    beside = (c + cols - 1) // cols + 1 - (c + 1) // cols
    pl.semaphore_wait(barrier, len(peers) + beside)

    def send(src, dst, send_sem, recv_sem, device):
        return pltpu.make_async_remote_copy(
            src_ref=src,
            dst_ref=dst,
            send_sem=send_sem,
            recv_sem=recv_sem,
            device_id=device,
            device_id_type=pl.DeviceIdType.MESH,
        )

    def rows_of(p, part):
        first, size = (half - (p + 1) * count, count) if p < full else (half, 8)
        if part is not None and p < full:
            first, size = first + part * (size // 2), size // 2
        return pl.ds(first, size)

    def place(dev, p, part=None):
        return all_ref.at[dev, rows_of(p, part)]

    def source(p):
        return rev_ref if p < full else band_ref.at[pl.ds(0, 8)]

    def along(p, up, src):
        to = (c + 1) % cols if up else (c - 1 + cols) % cols
        return send(src, place(d, p), z_send.at[p, int(up)], z_recv.at[p], (d, to))

    def hops(p):
        for j in range(1, chips // 2 + 1):
            for way in (1, -1):
                if 2 * j < chips:
                    yield j, way, None
                elif p < full:
                    yield j, way, 0 if way == 1 else 1
                elif way == 1:
                    yield j, way, None

    def across(p, j, way, part, src=None):
        dev = at(-way * (j - 1))
        src = place(dev, p, part) if src is None else src
        which = 2 * j + (way + 1) // 2
        return send(src, place(dev, p, part), p_send.at[p, which], p_recv.at[p, which], (at(way), c))

    def pair(p, j, way, part, src=None):
        dev = at(-way * j)
        src = place(dev, p, part) if src is None else src
        which = 2 * j + (way + 1) // 2
        return send(src, place(dev, p, part), c_send.at[p, which], c_recv.at[p, which], (partner, c))

    def own(p):
        return pltpu.make_async_copy(source(p), place(d, p), own_sem)

    def first_hops(p, src):
        for j, way, part in hops(p):
            if j == 1:
                across(p, 1, way, part, src).start()
        pair(p, 0, 1, None, src).start()

    rows_dev = eig_ref.shape[0]
    halos = []
    end = sum(takes)
    for hop, take in enumerate(takes, 1):
        halos.append(
            send(
                eig_ref.at[pl.ds(rows_dev - take, take)],
                above_ref.at[pl.ds(end - take, take)],
                e_send.at[hop],
                e_recv.at[hop],
                ((d + hop) % devices, c),
            )
        )
        end -= take
    halos.append(
        send(eig_ref.at[pl.ds(0, 8)], under_ref, e_send.at[0], e_recv.at[0], ((d - 1 + devices) % devices, c))
    )

    for p in range(pieces):

        @pl.when(c == p)
        def _():
            @pl.when(c < cols - 1)
            def _():
                along(p, True, source(p)).start()

            @pl.when(c > 0)
            def _():
                along(p, False, source(p)).start()

            first_hops(p, source(p))
            own(p).start()

    def receive(p):
        @pl.when(c != p)
        def _():
            along(p, True, place(d, p)).wait_recv()

            @pl.when((c > p) & (c < cols - 1))
            def _():
                along(p, True, place(d, p)).start()

            @pl.when((c < p) & (c > 0))
            def _():
                along(p, False, place(d, p)).start()

            first_hops(p, place(d, p))

    def relay(p, level):
        for j, way, part in hops(p):
            if j == level:
                across(p, j, way, part).wait_recv()
                for j2, way2, part2 in hops(p):
                    if j2 == j + 1 and way2 == way:
                        across(p, j2, way, part2).start()
                pair(p, j, way, part).start()

    for p in reversed(range(pieces)):
        receive(p)
    for halo in halos:
        halo.start()
    for level in range(1, chips // 2 + 1):
        for p in reversed(range(pieces)):
            relay(p, level)
    for p in range(pieces):

        @pl.when(c == p)
        def _():
            own(p).wait()

        @pl.when((c >= p) & (c < cols - 1))
        def _():
            along(p, True, place(d, p)).wait_send()

        @pl.when((c <= p) & (c > 0))
        def _():
            along(p, False, place(d, p)).wait_send()

        for j, way, part in hops(p):
            across(p, j, way, part).wait_send()
            pair(p, j, way, part).wait()
        pair(p, 0, 1, None).wait()
    for halo in halos:
        halo.wait()


def body(band_diagonals, eigenvectors):
    piece_count, rows_dev = band_diagonals.shape
    cols = lax.axis_size("cols")
    double = piece_count * cols
    half = double // 2
    blocks_dev = rows_dev // half
    devices = lax.axis_size("band")
    blocks = blocks_dev * devices
    sweeps = SWEEPS
    halo = sweeps
    columns = eigenvectors.shape[1]
    f32 = jnp.float32
    vmem = pl.BlockSpec(memory_space=pltpu.VMEM)

    takes = []
    while sum(takes) < halo * half:
        takes.append(min(halo * half - sum(takes), rows_dev))
    pieces = half // piece_count + 1
    dma = pltpu.SemaphoreType.DMA
    band, above, under = pl.pallas_call(
        functools.partial(gather_kernel, half, devices, cols, takes),
        out_shape=(
            jax.ShapeDtypeStruct((devices, half + 8, rows_dev), f32),
            jax.ShapeDtypeStruct((halo * half, columns), f32),
            jax.ShapeDtypeStruct((8, columns), f32),
        ),
        in_specs=[vmem] * 2,
        out_specs=(vmem,) * 3,
        scratch_shapes=[
            pltpu.VMEM((piece_count, rows_dev), f32),
            [
                dma((pieces, 2)),
                dma((pieces,)),
                dma((pieces, devices + 2)),
                dma((pieces, devices + 2)),
                dma((pieces, devices + 2)),
                dma((pieces, devices + 2)),
                dma((len(takes) + 1,)),
                dma((len(takes) + 1,)),
                dma,
            ]
        ],
        compiler_params=pltpu.CompilerParams(collective_id=0, has_side_effects=True),
    )(band_diagonals, eigenvectors)

    slots = blocks + 3
    scratch = (
        [pltpu.VMEM((slots, half, half), f32)] * (2 * (sweeps + 1))
        + [pltpu.VMEM((slots, half, half), f32)] * sweeps
        + [pltpu.VMEM((slots, 8, half), f32)] * sweeps
        + [pltpu.VMEM((half, half), f32)] * sweeps
        + [
            pltpu.VMEM((8, half), f32),
            pltpu.VMEM((half, half), f32),
            pltpu.VMEM((double, half), f32),
        ]
    )
    return pl.pallas_call(
        functools.partial(chase_kernel, blocks, half, blocks_dev, halo, piece_count, sweeps),
        out_shape=(
            jax.ShapeDtypeStruct((piece_count, rows_dev), f32),
            jax.ShapeDtypeStruct((rows_dev, columns), f32),
        ),
        in_specs=[vmem] * 4,
        out_specs=(vmem, vmem),
        scratch_shapes=scratch,
        compiler_params=pltpu.CompilerParams(vmem_limit_bytes=62 * 1024 * 1024),
    )(band, above, eigenvectors, under)


def solution(mesh):
    return jax.shard_map(
        body,
        mesh=mesh,
        in_specs=(P("cols", "band"), P("band", "cols")),
        out_specs=(P("cols", "band"), P("band", "cols")),
        check_vma=False,
    )
```
